256 devices in a mesh: blk: 256 (over z, x, y, core).
Axes of the slice: x: 4, y: 4, z: 8, core: 2. Of those that a mesh axis runs over, the one named last changes fastest.
Arguments:
- blocks: float32 [4, 4096, 256, 128], P(None, 'blk'), may hold values from -6 to 6
- first: float32 [4096, 256], P('blk'), may hold values from -2.4 to 2.4
- second: float32 [65536, 256], P('blk'), may hold values from -2.4 to 2.4
- third: float32 [32768, 256], P('blk'), may hold values from -2.4 to 2.4
Outputs:
- first_final: float32 [4096, 256], P('blk')
- second_final: float32 [65536, 256], P('blk')
- third_final: float32 [32768, 256], P('blk')
The draws below stay inside these ranges and needn't reach their ends.
All inputs are finite; a program needn't handle non-finite values.
Results may differ from the reference program's by a relative error of at most 0.0003.
Values sent between devices are 32-bit elements; how exact they have to be, the bound alone decides.
No kernel may reach another device: no remote copies, remote signals or barrier semaphores. Data moves between devices by JAX's collectives and lax.ppermute only.
A program may use at most 64 MiB of HBM per device.

```python
import jax
import jax.numpy as jnp
from jax import lax

RANK = 256
STRATA = 4
I_DEV = 16
J_DEV = 256
K_DEV = 128
BLOCKS = 256
I_ROWS = 4096
J_ROWS = 65536
K_ROWS = 32768


def levels(stream_key, dims, shards, smallest, top_value):
    gain = 1.0
    for dim, blocks in shards:
        steps = jax.random.uniform(jax.random.fold_in(jax.random.fold_in(stream_key, 6), dim), (blocks,), jnp.float32, smallest / len(shards), top_value / len(shards))
        gain = gain * jnp.repeat(jnp.exp(steps), dims[dim] // blocks).reshape((-1,) + (1,) * (len(dims) - 1 - dim))
    return gain


def noise(key, dims, scale, most, cuts=(), kind=jnp.bfloat16):
    result = scale * jax.random.normal(key, dims, jnp.float32)
    if cuts:
        result = result * levels(key, dims, cuts, -0.22, 0.18)
    return jnp.clip(result, -most, most).astype(kind)


def setup_inputs(seed: int = 0) -> dict:
    key_list = jax.random.split(jax.random.key(seed), 5)
    return {
        "blocks": noise(key_list[0], (STRATA, I_ROWS, J_DEV, K_DEV), 1.0, 6.0, ((1, 256),), jnp.float32),
        "first": noise(key_list[1], (I_ROWS, RANK), 0.4, 2.4, ((0, 256),), jnp.float32),
        "second": noise(key_list[2], (J_ROWS, RANK), 0.4, 2.4, ((0, 256),), jnp.float32),
        "third": noise(key_list[3], (K_ROWS, RANK), 0.4, 2.4, ((0, 256),), jnp.float32),
    }


momentum = 0.5
step_scale = 8.0


def gradients(target, first_block, second_block, third_block):
    first_rows = first_block.shape[0]
    second_rows = second_block.shape[0]
    paired = (first_block[:, None, :] * second_block[None, :, :]).reshape(first_rows * second_rows, -1)
    modeled = jnp.dot(paired, third_block.T, precision=lax.Precision.HIGHEST)
    misfit = modeled - target.reshape(first_rows * second_rows, -1)
    contracted = jnp.dot(misfit, third_block, precision=lax.Precision.HIGHEST).reshape(first_rows, second_rows, -1)
    grad_first = jnp.sum(contracted * second_block[None, :, :], axis=1)
    grad_second = jnp.sum(contracted * first_block[:, None, :], axis=0)
    grad_third = lax.dot_general(misfit, paired, (((0,), (0,)), ((), ())), precision=lax.Precision.HIGHEST)
    return grad_first, grad_second, grad_third


def advance(factor, velocity, gradient, rate):
    keep = momentum * velocity
    step = rate * gradient
    return (factor + keep) - step, keep - step


def device_grads(parts):
    return gradients(parts[0], parts[1], parts[2], parts[3])


def reference(blocks, first, second, third):
    first_blk = first.reshape(BLOCKS, I_DEV, RANK)
    second_blk = second.reshape(BLOCKS, J_DEV, RANK)
    third_blk = third.reshape(BLOCKS, K_DEV, RANK)
    vel_first = jnp.zeros_like(first_blk)
    vel_second = jnp.zeros_like(second_blk)
    vel_third = jnp.zeros_like(third_blk)
    rate_first = step_scale / (J_DEV * K_DEV)
    rate_second = step_scale / (I_DEV * K_DEV)
    rate_third = step_scale / (I_DEV * J_DEV)
    for stratum in range(STRATA):
        second_now = jnp.roll(second_blk, -stratum, axis=0)
        third_now = jnp.roll(third_blk, -3 * stratum, axis=0)
        target = blocks[stratum].reshape(BLOCKS, I_DEV, J_DEV, K_DEV)
        grad_first, grad_second, grad_third = lax.map(device_grads, (target, first_blk, second_now, third_now))
        grad_second = jnp.roll(grad_second, stratum, axis=0)
        grad_third = jnp.roll(grad_third, 3 * stratum, axis=0)
        first_blk, vel_first = advance(first_blk, vel_first, grad_first, rate_first)
        second_blk, vel_second = advance(second_blk, vel_second, grad_second, rate_second)
        third_blk, vel_third = advance(third_blk, vel_third, grad_third, rate_third)
    return (first_blk.reshape(I_ROWS, RANK), second_blk.reshape(J_ROWS, RANK), third_blk.reshape(K_ROWS, RANK))
```

```python
import jax
import jax.numpy as jnp
from jax import lax
from jax.experimental import pallas as pl
from jax.experimental.pallas import tpu as pltpu
from jax.sharding import PartitionSpec as P


momentum = 0.5
step_scale = 8.0
F32 = jnp.float32
BF16 = jnp.bfloat16


def shifted(array, axis, by):
    count = lax.axis_size(axis)
    return lax.ppermute(array, axis, [(i, (i + by) % count) for i in range(count)])


def split(x):
    high = x.astype(BF16)
    return high, (x - high.astype(F32)).astype(BF16)


def dot(a, b):
    return jnp.dot(a, b, preferred_element_type=F32)


def dot3(a, b):
    return dot(a[0], b[0]) + dot(a[0], b[1]) + dot(a[1], b[0])


def gram(x):
    return dot3(split(x.T), split(x))


def vmem(n):
    return [pl.BlockSpec(memory_space=pltpu.VMEM)] * n


def prepare_kernel(s, first_rows, blocks, natural_h, natural_l, turned_h, turned_l, buf, sem):
    pairs = first_rows // 2
    third_rows = buf.shape[-1]

    def fetch(p):
        return pltpu.make_async_copy(blocks.at[s, pl.ds(2 * p, 2)], buf.at[p], sem.at[p])

    for p in range(pairs):
        fetch(p).start()

    def body(p, _):
        fetch(p).wait()
        for h in range(2):
            t = buf[p, h]
            high, low = split(t)
            cols = slice(h * third_rows, (h + 1) * third_rows)
            natural_h[p, :, cols] = high
            natural_l[p, :, cols] = low
            high, low = split(t.T)
            rows = pl.ds(pl.multiple_of((2 * p + h) * third_rows, third_rows), third_rows)
            turned_h[rows, :] = high
            turned_l[rows, :] = low
        return 0

    lax.fori_loop(0, pairs, body, 0)


def prepare(s, blocks):
    _, first_rows, second_rows, third_rows = blocks.shape
    pairs = first_rows // 2
    natural = jax.ShapeDtypeStruct((pairs, second_rows, 2 * third_rows), BF16)
    turned = jax.ShapeDtypeStruct((first_rows * third_rows, second_rows), BF16)
    return pl.pallas_call(
        lambda *refs: prepare_kernel(s, first_rows, *refs),
        out_shape=(natural, natural, turned, turned),
        in_specs=[pl.BlockSpec(memory_space=pltpu.HBM)],
        out_specs=tuple(vmem(4)),
        scratch_shapes=[
            pltpu.VMEM((pairs, 2, second_rows, third_rows), F32),
            pltpu.SemaphoreType.DMA((pairs,)),
        ],
        compiler_params=pltpu.CompilerParams(vmem_limit_bytes=16 << 20),
        cost_estimate=pl.CostEstimate(flops=0, bytes_accessed=4 << 20, transcendentals=0),
        name="prepare",
    )(pltpu.with_memory_space_constraint(blocks, pltpu.HBM))


def second_side_kernel(first, third, natural_h, natural_l, target_second, gram_first, gram_third):
    pairs = natural_h.shape[0]
    c = third[...]
    gram_first[...] = gram(first[...])
    gram_third[...] = gram(c)
    target_second[...] = jnp.zeros_like(target_second)

    def body(p, _):
        paired = jnp.concatenate([first[pl.ds(2 * p, 1), :] * c, first[pl.ds(2 * p + 1, 1), :] * c], axis=0)
        target_second[...] += dot3((natural_h[p], natural_l[p]), split(paired))
        return 0

    lax.fori_loop(0, pairs, body, 0)


def second_side(first, third, natural_h, natural_l):
    rank = first.shape[1]
    second_rows = natural_h.shape[1]
    square = jax.ShapeDtypeStruct((rank, rank), F32)
    return pl.pallas_call(
        second_side_kernel,
        out_shape=(jax.ShapeDtypeStruct((second_rows, rank), F32), square, square),
        in_specs=vmem(4),
        out_specs=tuple(vmem(3)),
        compiler_params=pltpu.CompilerParams(vmem_limit_bytes=16 << 20),
        cost_estimate=pl.CostEstimate(flops=1 << 30, bytes_accessed=4 << 20, transcendentals=0),
        name="second_side",
    )(first, third, natural_h, natural_l)


def advance(factor, velocity, gradient, rate):
    keep = momentum * velocity
    step = rate * gradient
    return (factor + keep - step, keep - step)


def update_kernel(rates, groups, turned_h, turned_l, target_second, gram_first, gram_third, *refs):
    ins, outs, (contracted, grad_first) = refs[:6], refs[6:12], refs[12:]
    a, b, c = (ref[...] for ref in ins[:3])
    split_b = split(b)
    gram_second = dot3(split(b.T), split_b)
    first_rows, third_rows = a.shape[0], c.shape[0]
    size = first_rows // groups

    g_second = dot3(split_b, split(gram_first[...] * gram_third[...])) - target_second[...]
    outs[1][...], outs[4][...] = advance(b, ins[4][...], g_second, rates[1])

    def body(g, g_third):
        rows = pl.ds(pl.multiple_of(g * size * third_rows, size * third_rows), size * third_rows)
        contracted[...] = dot3((turned_h[rows, :], turned_l[rows, :]), split_b)
        for n in range(size):
            part = contracted[n * third_rows : (n + 1) * third_rows, :]
            row = pl.ds(g * size + n, 1)
            grad_first[row, :] = jnp.sum(part * c, axis=0, keepdims=True)
            g_third = g_third + part * ins[0][row, :]
        return g_third

    g_third = lax.fori_loop(0, groups, body, jnp.zeros_like(c))
    g_third = dot3(split(c), split(gram_first[...] * gram_second)) - g_third
    outs[2][...], outs[5][...] = advance(c, ins[5][...], g_third, rates[2])
    g_first = dot3(split(a), split(gram_second * gram_third[...])) - grad_first[...]
    outs[0][...], outs[3][...] = advance(a, ins[3][...], g_first, rates[0])


def update(rates, turned, sides, factors, velocities):
    groups = 4
    shapes = [jax.ShapeDtypeStruct(x.shape, F32) for x in (*factors, *velocities)]
    first_rows, rank = factors[0].shape
    third_rows = factors[2].shape[0]
    out = pl.pallas_call(
        lambda *refs: update_kernel(rates, groups, *refs),
        out_shape=tuple(shapes),
        in_specs=vmem(11),
        out_specs=tuple(vmem(6)),
        scratch_shapes=[
            pltpu.VMEM((first_rows // groups * third_rows, rank), F32),
            pltpu.VMEM((first_rows, rank), F32),
        ],
        compiler_params=pltpu.CompilerParams(vmem_limit_bytes=16 << 20),
        cost_estimate=pl.CostEstimate(flops=1 << 30, bytes_accessed=4 << 20, transcendentals=0),
        name="update",
    )(*turned, *sides, *factors, *velocities)
    return out[:3], out[3:]


def shards(blocks, first, second, third):
    strata = blocks.shape[0]
    first_rows = first.shape[0]
    second_rows = second.shape[0]
    third_rows = third.shape[0]
    rates = (
        step_scale / (second_rows * third_rows),
        step_scale / (first_rows * third_rows),
        step_scale / (first_rows * second_rows),
    )
    vel_first, vel_second, vel_third = (jnp.zeros_like(x) for x in (first, second, third))
    source = blocks
    for stratum in range(strata):
        natural_h, natural_l, turned_h, turned_l = prepare(stratum, source)
        sides = second_side(first, third, natural_h, natural_l)
        (first, second, third), (vel_first, vel_second, vel_third) = update(
            rates, (turned_h, turned_l), sides, (first, second, third), (vel_first, vel_second, vel_third)
        )
        if stratum + 1 < strata:
            source, first = lax.optimization_barrier((blocks, first))
            third = shifted(third, "blk", -3)
            second = shifted(second, "blk", -1)
            vel_third = shifted(vel_third, "blk", -3)
            vel_second = shifted(vel_second, "blk", -1)
    third = shifted(third, "blk", 3 * (strata - 1))
    second = shifted(second, "blk", strata - 1)
    return (first, second, third)


def solution(mesh):
    placed = (P(None, "blk", None, None), P("blk", None), P("blk", None), P("blk", None))
    return jax.shard_map(
        shards,
        mesh=mesh,
        in_specs=placed,
        out_specs=(P("blk", None), P("blk", None), P("blk", None)),
        check_vma=False,
    )
```

```python
import jax
import jax.numpy as jnp
from jax import lax
from jax.experimental import pallas as pl
from jax.experimental.pallas import tpu as pltpu
from jax.sharding import PartitionSpec as P


momentum = 0.5
step_scale = 8.0
F32 = jnp.float32
BF16 = jnp.bfloat16


def sent(array, by):
    count = lax.axis_size("blk")
    return lax.ppermute(array, "blk", [(i, (i + by) % count) for i in range(count)])


def split(x):
    high = x.astype(BF16)
    return high, (x - high.astype(F32)).astype(BF16)


def dot(a, b):
    return jnp.dot(a, b, preferred_element_type=F32)


def dot3(a, b):
    return dot(a[0], b[0]) + dot(a[0], b[1]) + dot(a[1], b[0])


def gram(x):
    return dot3(split(x.T), split(x))


def vmem(n):
    return [pl.BlockSpec(memory_space=pltpu.VMEM)] * n


def like(*shape, dtype=F32):
    return jax.ShapeDtypeStruct(shape, dtype)


def kernel(body, out_shape, operands, in_specs=None, scratch_shapes=()):
    return pl.pallas_call(
        body,
        out_shape=tuple(out_shape),
        in_specs=in_specs or vmem(len(operands)),
        out_specs=tuple(vmem(len(out_shape))),
        scratch_shapes=scratch_shapes,
        compiler_params=pltpu.CompilerParams(vmem_limit_bytes=16 << 20),
        cost_estimate=pl.CostEstimate(flops=1 << 30, bytes_accessed=4 << 20, transcendentals=0),
    )(*operands)


def prepare(s, blocks):
    _, first_rows, second_rows, third_rows = blocks.shape
    pairs = first_rows // 2

    def body(target, natural_h, natural_l, turned_h, turned_l, buf, sem):
        def fetch(p):
            return pltpu.make_async_copy(target.at[s, pl.ds(2 * p, 2)], buf.at[p], sem.at[p])

        for p in range(pairs):
            fetch(p).start()
        for p in range(pairs):
            fetch(p).wait()
            for h in range(2):
                t = buf[p, h]
                span = slice((2 * p + h) * third_rows, (2 * p + h + 1) * third_rows)
                natural_h[:, span], natural_l[:, span] = split(t)
                turned_h[span, :], turned_l[span, :] = split(t.T)

    wide = first_rows * third_rows
    natural, turned = like(second_rows, wide, dtype=BF16), like(wide, second_rows, dtype=BF16)
    return kernel(
        body,
        (natural, natural, turned, turned),
        (pltpu.with_memory_space_constraint(blocks, pltpu.HBM),),
        in_specs=[pl.BlockSpec(memory_space=pltpu.HBM)],
        scratch_shapes=[
            pltpu.VMEM((pairs, 2, second_rows, third_rows), F32),
            pltpu.SemaphoreType.DMA((pairs,)),
        ],
    )


def second_side(first, third, older, natural_h, natural_l):
    first_rows, rank = first.shape
    third_rows = third.shape[0]
    second_rows, wide = natural_h.shape
    chunks = 4

    def body(a, c, *refs):
        if older is not None:
            o, refs = refs[0], refs[1:]
            c_now = c[...] - momentum * o[...]
        else:
            c_now = c[...]
        nat_h, nat_l, target_second, gram_first, gram_third = refs[:5]
        pair_h, pair_l = refs[-2:]
        if older is not None:
            refs[5][...] = c_now
        total = None
        for n in range(chunks):
            size = first_rows // chunks
            for i in range(n * size, (n + 1) * size):
                span = slice(i * third_rows, (i + 1) * third_rows)
                pair_h[span, :], pair_l[span, :] = split(a[i : i + 1, :] * c_now)
            span = slice(n * wide // chunks, (n + 1) * wide // chunks)
            part = dot3((nat_h[:, span], nat_l[:, span]), (pair_h[span, :], pair_l[span, :]))
            total = part if total is None else total + part
        target_second[...] = total
        gram_first[...] = gram(a[...])
        gram_third[...] = gram(c_now)

    olds = () if older is None else (older,)
    out = kernel(
        body,
        (like(second_rows, rank), like(rank, rank), like(rank, rank)) + ((like(third_rows, rank),) if olds else ()),
        (first, third, *olds, natural_h, natural_l),
        scratch_shapes=[pltpu.VMEM((wide, rank), BF16)] * 2,
    )
    return out if olds else (*out, third)


def update(s, strata, rates, turned, target_second, grams, factors, vel_first, old_second):
    first_rows, rank = factors[0].shape
    third_rows = factors[2].shape[0]
    ahead = 1.0 if s == 0 else 1.0 + momentum
    last = s + 1 == strata

    def body(turned_h, turned_l, t_second, gram_first, gram_third, *refs):
        a, b, c = (ref[...] for ref in refs[:3])
        rest = list(refs[3:])
        vel = momentum * rest.pop(0)[...] if s else None
        old = rest.pop(0)[...] if old_second is not None else None
        new_first, new_second, new_third = rest[:3]
        contracted = rest[-1]
        split_b = split(b)
        contracted[...] = dot3((turned_h[...], turned_l[...]), split_b)
        gram_second = dot3(split(b.T), split_b)

        g_second = dot3(split_b, split(gram_first[...] * gram_third[...])) - t_second[...]
        base = ahead * b if old is None else ahead * b - momentum * old
        new_second[...] = base - rates[1] * g_second

        g_third = jnp.zeros_like(c)
        rows = []
        for i in range(first_rows):
            part = contracted[i * third_rows : (i + 1) * third_rows, :]
            rows.append(jnp.sum(part * c, axis=0, keepdims=True))
            g_third = g_third + part * refs[0][i : i + 1, :]
        g_third = dot3(split(c), split(gram_first[...] * gram_second)) - g_third
        new_third[...] = ahead * c - rates[2] * g_third
        g_first = dot3(split(a), split(gram_second * gram_third[...])) - jnp.concatenate(rows, axis=0)
        step = rates[0] * g_first
        new_first[...] = a - step if vel is None else a + vel - step
        if not last:
            rest[3][...] = -step if vel is None else vel - step

    operands = (*turned, target_second, *grams, *factors)
    operands += (vel_first,) if s else ()
    operands += () if old_second is None else (old_second,)
    shapes = [pltpu.VMEM(factors[0].shape, F32) if last else like(*factors[0].shape)]
    shapes += [like(*x.shape) for x in factors[1:]] + ([] if last else [like(first_rows, rank)])
    return kernel(body, shapes, operands, scratch_shapes=[pltpu.VMEM((first_rows * third_rows, rank), F32)])


def shards(blocks, first, second, third):
    strata = 4
    first_rows = first.shape[0]
    second_rows = second.shape[0]
    third_rows = third.shape[0]
    rates = (
        step_scale / (second_rows * third_rows),
        step_scale / (first_rows * third_rows),
        step_scale / (first_rows * second_rows),
    )
    vel = None
    home_third = third
    old_second = old_third = None
    older = {}
    for s in range(strata):
        natural_h, natural_l, *turned = prepare(s, blocks)
        if s == 0:
            older["b1"] = sent(second, -1)
            older["c2"] = sent(third, -6)
        old_second, old_third = older.get(f"b{s}"), older.get(f"c{s}")
        target_second, *grams, third = second_side(first, third, old_third, natural_h, natural_l)
        first, second, third, *vel = update(
            s,
            strata,
            rates,
            turned,
            target_second,
            grams,
            (first, second, third),
            vel and vel[0],
            old_second,
        )
        if s == 0:
            older["b2"] = sent(second, -2)
            older["c3"] = sent(third, -9)
        if s == 1:
            back_second = sent(second, 1)
            back_third = sent(third, 3)
        if s + 1 < strata:
            third = sent(third, -3)
            second = sent(second, -1)
    third = sent(third, 3 * (strata - 1))
    second = sent(second, strata - 1)
    second = second - momentum * back_second
    third = third - momentum * (back_third - momentum * home_third)
    return (first, second, third)


def solution(mesh):
    placed = (P(None, "blk", None, None), P("blk", None), P("blk", None), P("blk", None))

    return jax.shard_map(
        shards,
        mesh=mesh,
        in_specs=placed,
        out_specs=(P("blk", None), P("blk", None), P("blk", None)),
        check_vma=False,
    )
```

```python
import jax
import jax.numpy as jnp
from jax import lax
from jax.experimental import pallas as pl
from jax.experimental.pallas import tpu as pltpu
from jax.sharding import PartitionSpec as P


momentum = 0.5
step_scale = 8.0
F32 = jnp.float32
BF16 = jnp.bfloat16


def sent(array, by):
    count = lax.axis_size("blk")
    return lax.ppermute(array, "blk", [(i, (i + by) % count) for i in range(count)])


def split(x):
    high = x.astype(BF16)
    return high, (x - high.astype(F32)).astype(BF16)


def dot(a, b):
    return jnp.dot(a, b, preferred_element_type=F32)


def dot3(a, b):
    return dot(a[0], b[0]) + dot(a[0], b[1]) + dot(a[1], b[0])


def turned_dot3(a, b):
    def turned_dot(x, y):
        return lax.dot_general(x, y, (((0,), (0,)), ((), ())), preferred_element_type=F32)

    return turned_dot(a[0], b[0]) + turned_dot(a[0], b[1]) + turned_dot(a[1], b[0])


def gram(x):
    return dot3(split(x.T), split(x))


def vmem(n):
    return [pl.BlockSpec(memory_space=pltpu.VMEM)] * n


def like(*shape, dtype=F32):
    return jax.ShapeDtypeStruct(shape, dtype)


def kernel(body, out_shape, operands, in_specs=None, scratch_shapes=()):
    return pl.pallas_call(
        body,
        out_shape=tuple(out_shape),
        in_specs=in_specs or vmem(len(operands)),
        out_specs=tuple(vmem(len(out_shape))),
        scratch_shapes=scratch_shapes,
        compiler_params=pltpu.CompilerParams(vmem_limit_bytes=16 << 20),
        cost_estimate=pl.CostEstimate(flops=1 << 30, bytes_accessed=4 << 20, transcendentals=0),
    )(*operands)


def prepare(s, blocks):
    _, first_rows, second_rows, third_rows = blocks.shape
    pairs = first_rows // 2

    def body(target, high, low, buf, sem):
        def fetch(p):
            return pltpu.make_async_copy(target.at[s, pl.ds(2 * p, 2)], buf.at[p], sem.at[p])

        for p in range(pairs):
            fetch(p).start()
        for p in range(pairs):
            fetch(p).wait()
            for h in range(2):
                span = slice((2 * p + h) * third_rows, (2 * p + h + 1) * third_rows)
                high[:, span], low[:, span] = split(buf[p, h])

    shape = like(second_rows, first_rows * third_rows, dtype=BF16)
    return kernel(
        body,
        (shape, shape),
        (pltpu.with_memory_space_constraint(blocks, pltpu.HBM),),
        in_specs=[pl.BlockSpec(memory_space=pltpu.HBM)],
        scratch_shapes=[
            pltpu.VMEM((pairs, 2, second_rows, third_rows), F32),
            pltpu.SemaphoreType.DMA((pairs,)),
        ],
    )


def second_side(first, third, older, target):
    first_rows, rank = first.shape
    third_rows = third.shape[0]
    second_rows, wide = target[0].shape
    chunks = 4

    def body(a, c, *refs):
        if older is not None:
            o, refs = refs[0], refs[1:]
            c_now = c[...] - momentum * o[...]
        else:
            c_now = c[...]
        nat_h, nat_l, target_second, gram_first, gram_third = refs[:5]
        pair_h, pair_l = refs[-2:]
        if older is not None:
            refs[5][...] = c_now
        total = None
        for n in range(chunks):
            size = first_rows // chunks
            for i in range(n * size, (n + 1) * size):
                span = slice(i * third_rows, (i + 1) * third_rows)
                pair_h[span, :], pair_l[span, :] = split(a[i : i + 1, :] * c_now)
            span = slice(n * wide // chunks, (n + 1) * wide // chunks)
            part = dot3((nat_h[:, span], nat_l[:, span]), (pair_h[span, :], pair_l[span, :]))
            total = part if total is None else total + part
        target_second[...] = total
        gram_first[...] = gram(a[...])
        gram_third[...] = gram(c_now)

    olds = () if older is None else (older,)
    out = kernel(
        body,
        (like(second_rows, rank), like(rank, rank), like(rank, rank)) + ((like(third_rows, rank),) if olds else ()),
        (first, third, *olds, *target),
        scratch_shapes=[pltpu.VMEM((wide, rank), BF16)] * 2,
    )
    return out if olds else (*out, third)


def step_second(s, rate, target_second, grams, second, older):
    ahead = 1.0 if s == 0 else 1.0 + momentum

    def body(t_second, gram_first, gram_third, b_ref, *refs):
        b = b_ref[...]
        gradient = dot3(split(b), split(gram_first[...] * gram_third[...])) - t_second[...]
        base = ahead * b if older is None else ahead * b - momentum * refs[0][...]
        refs[-1][...] = base - rate * gradient

    olds = () if older is None else (older,)
    (new,) = kernel(body, (like(*second.shape),), (target_second, *grams, second, *olds))
    return new


def step_others(s, strata, rates, target, grams, factors, vel_first):
    first_rows, rank = factors[0].shape
    third_rows = factors[2].shape[0]
    ahead = 1.0 if s == 0 else 1.0 + momentum
    last = s + 1 == strata

    def body(target_h, target_l, gram_first, gram_third, *refs):
        a, b, c = (ref[...] for ref in refs[:3])
        vel = momentum * refs[3][...] if s else None
        new_first, new_third, *new_vel = refs[4:] if s else refs[3:]
        split_b = split(b)
        gram_second = dot3(split(b.T), split_b)
        g_third = jnp.zeros_like(c)
        rows = []
        for i in range(first_rows):
            span = slice(i * third_rows, (i + 1) * third_rows)
            part = turned_dot3((target_h[:, span], target_l[:, span]), split_b)
            rows.append(jnp.sum(part * c, axis=0, keepdims=True))
            g_third = g_third + part * refs[0][i : i + 1, :]
        g_third = dot3(split(c), split(gram_first[...] * gram_second)) - g_third
        new_third[...] = ahead * c - rates[2] * g_third
        g_first = dot3(split(a), split(gram_second * gram_third[...])) - jnp.concatenate(rows, axis=0)
        step = rates[0] * g_first
        new_first[...] = a - step if vel is None else a + vel - step
        if not last:
            new_vel[0][...] = -step if vel is None else vel - step

    shapes = [pltpu.VMEM(factors[0].shape, F32) if last else like(*factors[0].shape), like(third_rows, rank)]
    shapes += [] if last else [like(first_rows, rank)]
    return kernel(body, shapes, (*target, *grams, *factors, *((vel_first,) if s else ())))


def shards(blocks, first, second, third):
    strata = 4
    first_rows = first.shape[0]
    second_rows = second.shape[0]
    third_rows = third.shape[0]
    rates = (
        step_scale / (second_rows * third_rows),
        step_scale / (first_rows * third_rows),
        step_scale / (first_rows * second_rows),
    )
    vel = None
    home_third = third
    old_second = old_third = None
    older = {}
    for s in range(strata):
        target = prepare(s, blocks)
        if s == 0:
            older["b1"] = sent(second, -1)
            older["c2"] = sent(third, -6)
        came = second
        old_second, old_third = older.get(f"b{s}"), older.get(f"c{s}")
        target_second, *grams, third = second_side(first, third, old_third, target)
        new_second = step_second(s, rates[1], target_second, grams, second, old_second)
        first, third, *vel = step_others(
            s, strata, rates, target, grams, (first, second, third), vel and vel[0]
        )
        second = new_second
        if s == 0:
            older["c3"] = sent(third, -9)
        if s == 1:
            older["b2"] = sent(came, -1)
            back_second = sent(second, 1)
            back_third = sent(third, 3)
        if s + 1 < strata:
            third = sent(third, -3)
            second = sent(second, -1)
    third = sent(third, 3 * (strata - 1))
    second = sent(second, strata - 1)
    second = second - momentum * back_second
    third = third - momentum * (back_third - momentum * home_third)
    return (first, second, third)


def solution(mesh):
    placed = (P(None, "blk", None, None), P("blk", None), P("blk", None), P("blk", None))

    return jax.shard_map(
        shards,
        mesh=mesh,
        in_specs=placed,
        out_specs=(P("blk", None), P("blk", None), P("blk", None)),
        check_vma=False,
    )
```
